32 devices in a mesh: parts: 32 (over z, y, x, core).
Axes of the slice: x: 2, y: 2, z: 4, core: 2. Of those that a mesh axis runs over, the one named last changes fastest.
Arguments:
- rhs: float32 [216, 16384], P(None, 'parts'), may hold values from -60 to 90
- start: float32 [216, 16384], P(None, 'parts'), may hold values from -3.75 to 5.625
- spectrum_top: float32 [1], replicated, may hold values from 10 to 20
- elem_code: int32 [16384], P('parts'), may hold values from 0 to 2, as said below
- rec_elem: int32 [98304], P('parts'), may hold values from 0 to 511, as said below
- rec_dir: int32 [98304], P('parts'), may hold values from 0 to 5
- rec_sub: int32 [98304], P('parts'), may hold values from 0 to 5, as said below
- rec_peer: int32 [98304], P('parts'), may hold values from -1 to 31, as said below
- rec_index: int32 [98304], P('parts'), may hold values from 0 to 3071, as said below
- send_rec: int32 [262144], P('parts'), may hold values from 0 to 3071, as said below
Outputs:
- solution: float32 [216, 16384], P(None, 'parts')
- norms: float32 [3, 2], replicated
The draws below stay inside these ranges and needn't reach their ends.
Inputs may be any that keep to these rules, and one draw needn't show every extreme that they name: `elem_code`: 0 marks an empty slot, 1 a fine element, 2 a coarse element; a device's live slots come first. `rec_elem`: always a live element of the record's device. `rec_sub`: 0 to 3: a quarter of a coarse face facing a fine element; 4: the whole face; 5: an unused slot, which comes after the device's used records. `rec_peer`: -1 at the channel's ends and on unused slots. A partner is never more than 7 devices away; its face has the opposite direction, and the partner's partner is the record itself. `rec_index`: A record index on the same device, or a slot of the partner device's send list to this device. `send_rec`: entries of slots that no record names are arbitrary. At most 256 slots are named from one device to another, and some pair of devices uses all 256.
All inputs are finite; a program needn't handle non-finite values.
Results may differ from the reference program's by a relative error of at most 0.0003.
Values sent between devices are 32-bit elements; how exact they have to be, the bound alone decides.
A program may use at most 128 MiB of HBM per device.

```python
import math
import jax
import jax.numpy as jnp
import numpy as np
from jax import lax

NODES = 216
US = 8
LX_DEV = 1
LD = 4
ITERS = 3
ELEMS = 16384
N_PARTS = 32


def spread_bits(number):
    result = jnp.zeros_like(number)
    for bit_index in range(4):
        result = result | (number >> bit_index & 1) << 2 * bit_index
    return result


def gather_bits(number):
    result = jnp.zeros_like(number)
    for bit_index in range(4):
        result = result | (number >> 2 * bit_index & 1) << bit_index
    return result


def shuffle_group(sub_key):
    return jax.random.permutation(sub_key, LD).astype(jnp.int32)


def mesh_layout(key):
    units_dev = LX_DEV * US * US
    unit_total = N_PARTS * units_dev
    elem_dev = 8 * units_dev
    rec_dev = 48 * units_dev
    capacity = max(4 * US * US, 8 * LX_DEV * US)
    cross_span = 2 * US
    group_count = N_PARTS // LD
    length_span = group_count * LX_DEV
    far_reach = 2 * LD - 1
    group_keys = jax.random.split(jax.random.fold_in(key, 11), group_count)
    place_of = jax.vmap(shuffle_group)(group_keys)
    quadrant_of = jnp.argsort(place_of, axis=1).astype(jnp.int32)
    unit_id = jnp.arange(unit_total, dtype=jnp.int32)
    device_of = unit_id // units_dev
    coin_flip = jax.random.randint(jax.random.fold_in(key, 7), (unit_total,), 0, 5)
    refined = (coin_flip < 2) | (device_of < 2 * LD)
    local_unit = unit_id % units_dev
    morton = local_unit % (US * US)
    own_quadrant = quadrant_of[device_of // LD, device_of % LD]
    coord_x = device_of // LD * LX_DEV + local_unit // (US * US)
    coord_y = own_quadrant % 2 * US + gather_bits(morton)
    coord_z = own_quadrant // 2 * US + gather_bits(morton >> 1)

    def unit_at(pos_x, pos_y, pos_z):
        group_index = pos_x // LX_DEV
        quadrant = pos_y // US + 2 * (pos_z // US)
        device = group_index * LD + place_of[group_index, quadrant]
        inner_index = spread_bits(pos_y % US) | spread_bits(pos_z % US) << 1
        return device * units_dev + pos_x % LX_DEV * US * US + inner_index
    child_index = jnp.arange(8, dtype=jnp.int32)[None, :, None]
    direction = jnp.arange(6, dtype=jnp.int32)[None, None, :]
    axis_index = direction // 2
    face_side = direction % 2
    bit_x = child_index & 1
    bit_y = child_index >> 1 & 1
    bit_z = child_index >> 2 & 1
    bit_axis = jnp.where(axis_index == 0, bit_x, jnp.where(axis_index == 1, bit_y, bit_z))
    first_bit = jnp.where(axis_index == 0, bit_y, bit_x)
    second_bit = jnp.where(axis_index == 2, bit_y, bit_z)
    step_sign = 2 * face_side - 1
    near_x = coord_x[:, None, None] + step_sign * (axis_index == 0).astype(jnp.int32)
    near_y = (coord_y[:, None, None] + step_sign * (axis_index == 1).astype(jnp.int32)) % cross_span
    near_z = (coord_z[:, None, None] + step_sign * (axis_index == 2).astype(jnp.int32)) % cross_span
    outside = (near_x < 0) | (near_x >= length_span)
    near_unit = unit_at(jnp.clip(near_x, 0, length_span - 1), near_y, near_z)
    near_refined = refined[near_unit]
    own_refined = refined[:, None, None]
    internal = own_refined & (bit_axis != face_side)
    flip_child = child_index ^ 1 << axis_index
    coarse_slot = first_bit + 2 * second_bit
    facing = 1 - face_side
    low_bit = child_index & 1
    high_bit = child_index >> 1 & 1
    facing_child = jnp.where(axis_index == 0, facing + 2 * low_bit + 4 * high_bit, jnp.where(axis_index == 1, low_bit + 2 * facing + 4 * high_bit, low_bit + 2 * high_bit + 4 * facing))
    shape_all = (unit_total, 8, 6)
    partner_unit = jnp.where(internal, unit_id[:, None, None], near_unit)
    partner_child = jnp.where(own_refined, jnp.where(internal | near_refined, flip_child, coarse_slot), jnp.where(near_refined, facing_child, 0))
    boundary = jnp.logical_not(internal) & outside
    valid_mask = jnp.where(own_refined, True, (child_index == 0) | (child_index < 4) & near_refined & jnp.logical_not(outside))
    sub_code = jnp.where(own_refined | outside | jnp.logical_not(near_refined), 4, child_index)
    unit_size = jnp.where(refined, 8, 1).astype(jnp.int32)
    start_all = jnp.cumsum(unit_size) - unit_size
    elem_offset = start_all - start_all[device_of * units_dev]
    elem_local = elem_offset[:, None, None] + jnp.where(own_refined, child_index, 0)
    child_row = jnp.arange(8, dtype=jnp.int32)[None, :]
    elem_slot = device_of[:, None] * elem_dev + elem_offset[:, None] + child_row
    keep_slot = refined[:, None] | (child_row == 0)
    elem_value = jnp.broadcast_to(jnp.where(refined, 1, 2).astype(jnp.int32)[:, None], (unit_total, 8))
    elem_code = jnp.zeros((N_PARTS * elem_dev,), jnp.int32).at[jnp.where(keep_slot, elem_slot, N_PARTS * elem_dev).reshape(-1)].set(elem_value.reshape(-1), mode='drop')
    valid_flat = jnp.broadcast_to(valid_mask, shape_all).reshape(-1)
    bound_flat = jnp.broadcast_to(boundary, shape_all).reshape(-1)
    valid_count = valid_flat.astype(jnp.int32)
    before = jnp.cumsum(valid_count) - valid_count
    cand_total = unit_total * 48
    cand_device = jnp.arange(cand_total, dtype=jnp.int32) // rec_dev
    local_rec = before - before[cand_device * rec_dev]
    partner_cand = (jnp.broadcast_to(partner_unit, shape_all) * 48 + jnp.broadcast_to(partner_child, shape_all) * 6 + jnp.broadcast_to(direction ^ 1, shape_all)).reshape(-1)
    partner_cand = jnp.where(bound_flat, 0, partner_cand)
    partner_device = partner_cand // rec_dev
    remote = valid_flat & jnp.logical_not(bound_flat) & (partner_device != cand_device)
    offset = jnp.clip(partner_device - cand_device + far_reach, 0, 2 * far_reach)
    onehot = ((offset[:, None] == jnp.arange(2 * far_reach + 1, dtype=jnp.int32)[None, :]) & remote[:, None]).astype(jnp.int32)
    running = jnp.cumsum(onehot, axis=0) - onehot
    running = running - running[cand_device * rec_dev]
    send_slot = jnp.take_along_axis(running, offset[:, None], axis=1)[:, 0]
    target = jnp.where(valid_flat, cand_device * rec_dev + local_rec, N_PARTS * rec_dev)
    slot_total = N_PARTS * rec_dev
    rec_elem = jnp.zeros((slot_total,), jnp.int32).at[target].set(jnp.broadcast_to(elem_local, shape_all).reshape(-1), mode='drop')
    rec_dir = jnp.zeros((slot_total,), jnp.int32).at[target].set(jnp.broadcast_to(direction, shape_all).reshape(-1), mode='drop')
    rec_sub = jnp.full((slot_total,), 5, jnp.int32).at[target].set(jnp.broadcast_to(sub_code, shape_all).reshape(-1), mode='drop')
    rec_peer = jnp.full((slot_total,), -1, jnp.int32).at[target].set(jnp.where(bound_flat, -1, partner_device), mode='drop')
    index_value = jnp.where(bound_flat, 0, jnp.where(remote, send_slot[partner_cand], local_rec[partner_cand]))
    rec_index = jnp.zeros((slot_total,), jnp.int32).at[target].set(index_value, mode='drop')
    link_total = N_PARTS * N_PARTS * capacity
    link_slot = jnp.where(remote, (cand_device * N_PARTS + partner_device) * capacity + send_slot, link_total)
    send_rec = jnp.zeros((link_total,), jnp.int32).at[link_slot].set(local_rec, mode='drop')
    return (elem_code, rec_elem, rec_dir, rec_sub, rec_peer, rec_index, send_rec)


def draw_elem_code(key, part):
    return mesh_layout(jax.random.fold_in(key, 3))[0]


def draw_rec_elem(key, part):
    return mesh_layout(jax.random.fold_in(key, 3))[1]


def draw_rec_dir(key, part):
    return mesh_layout(jax.random.fold_in(key, 3))[2]


def draw_rec_sub(key, part):
    return mesh_layout(jax.random.fold_in(key, 3))[3]


def draw_rec_peer(key, part):
    return mesh_layout(jax.random.fold_in(key, 3))[4]


def draw_rec_index(key, part):
    return mesh_layout(jax.random.fold_in(key, 3))[5]


def draw_send_rec(key, part):
    return mesh_layout(jax.random.fold_in(key, 3))[6]


def field_draw(key, base_scale):
    column = jnp.arange(ELEMS, dtype=jnp.float32) / ELEMS
    rough = jnp.clip(jax.random.normal(key, (NODES, ELEMS), jnp.float32), -5.0, 5.0)
    return base_scale * (1.0 + 2.0 * column)[None, :] * rough


def draw_rhs(key, part):
    return field_draw(jax.random.fold_in(key, 21), 4.0)


def draw_start(key, part):
    return field_draw(jax.random.fold_in(key, 22), 0.25)


def setup_inputs(seed: int = 0) -> dict:
    splits = jax.random.split(jax.random.key(seed), 11)
    return {
        "rhs": draw_rhs(jax.random.fold_in(splits[10], 71), 0),
        "start": draw_start(jax.random.fold_in(splits[10], 71), 0),
        "spectrum_top": jnp.clip(jax.random.uniform(splits[2], (1,), jnp.float32, 10.0, 20.0), 10.0, 20.0),
        "elem_code": draw_elem_code(jax.random.fold_in(splits[10], 71), 0),
        "rec_elem": draw_rec_elem(jax.random.fold_in(splits[10], 71), 0),
        "rec_dir": draw_rec_dir(jax.random.fold_in(splits[10], 71), 0),
        "rec_sub": draw_rec_sub(jax.random.fold_in(splits[10], 71), 0),
        "rec_peer": draw_rec_peer(jax.random.fold_in(splits[10], 71), 0),
        "rec_index": draw_rec_index(jax.random.fold_in(splits[10], 71), 0),
        "send_rec": draw_send_rec(jax.random.fold_in(splits[10], 71), 0),
    }


PENALTY = 36.0
BOTTOM_RATIO = 8.0
HIGHEST = lax.Precision.HIGHEST

def lobatto_tables():
    root_seven = math.sqrt(7.0)
    inner_root = math.sqrt(1.0 / 3.0 - 2.0 * root_seven / 21.0)
    outer_root = math.sqrt(1.0 / 3.0 + 2.0 * root_seven / 21.0)
    points = (np.array([-1.0, -outer_root, -inner_root, inner_root, outer_root, 1.0]) + 1.0) / 2.0
    weights = np.array([1.0 / 15.0, (14.0 - root_seven) / 30.0, (14.0 + root_seven) / 30.0, (14.0 + root_seven) / 30.0, (14.0 - root_seven) / 30.0, 1.0 / 15.0]) / 2.0
    barycentric = np.array([1.0 / np.prod([points[j] - points[k] for k in range(6) if k != j]) for j in range(6)])
    derivative = np.zeros((6, 6))
    for i in range(6):
        for j in range(6):
            if i != j:
                derivative[i, j] = barycentric[j] / barycentric[i] / (points[i] - points[j])
        derivative[i, i] = -np.sum(derivative[i])
    halves = np.zeros((2, 6, 6))
    for which_half in range(2):
        targets = (points + which_half) / 2.0
        for i in range(6):
            for j in range(6):
                halves[which_half, i, j] = np.prod([(targets[i] - points[k]) / (points[j] - points[k]) for k in range(6) if k != j])
    column_sums = np.sum(derivative * derivative * weights[:, None], axis=0)
    stiff_diag = column_sums[:, None, None] * weights[None, :, None] * weights[None, None, :] + weights[:, None, None] * column_sums[None, :, None] * weights[None, None, :] + weights[:, None, None] * weights[None, :, None] * column_sums[None, None, :]
    return (weights, derivative, halves, stiff_diag.reshape(216))

def float_tables():
    weights, derivative, halves, stiff_diag = lobatto_tables()
    return (jnp.asarray(weights, dtype=jnp.float32), jnp.asarray(derivative, dtype=jnp.float32), jnp.asarray(halves, dtype=jnp.float32), jnp.asarray(stiff_diag, dtype=jnp.float32))

def face_traces(nodal_field, inv_size, derivative):
    values = []
    normals = []
    for direction in range(6):
        axis_index = direction // 2
        layer_index = 5 * (direction % 2)
        orientation = 2.0 * (direction % 2) - 1.0
        slope_row = derivative[layer_index]
        if axis_index == 0:
            face_value = nodal_field[layer_index]
            normal = jnp.einsum('m,mjke->jke', slope_row, nodal_field, precision=HIGHEST)
        elif axis_index == 1:
            face_value = nodal_field[:, layer_index]
            normal = jnp.einsum('m,imke->ike', slope_row, nodal_field, precision=HIGHEST)
        else:
            face_value = nodal_field[:, :, layer_index]
            normal = jnp.einsum('m,ijme->ije', slope_row, nodal_field, precision=HIGHEST)
        values.append(face_value.reshape(36, -1))
        normals.append((normal * (orientation * inv_size)).reshape(36, -1))
    return (jnp.concatenate(values, axis=1), jnp.concatenate(normals, axis=1))

def lift_faces(face_value, face_slope, inv_size, derivative, elem_count):
    result = jnp.zeros((6, 6, 6, elem_count), jnp.float32)
    for direction in range(6):
        axis_index = direction // 2
        layer_index = 5 * (direction % 2)
        orientation = 2.0 * (direction % 2) - 1.0
        slope_row = derivative[layer_index]
        part_value = face_value[:, direction * elem_count:(direction + 1) * elem_count].reshape(6, 6, elem_count)
        part_slope = face_slope[:, direction * elem_count:(direction + 1) * elem_count].reshape(6, 6, elem_count)
        part_slope = part_slope * (orientation * inv_size)
        if axis_index == 0:
            result = result.at[layer_index].add(part_value)
            result = result + jnp.einsum('m,jke->mjke', slope_row, part_slope, precision=HIGHEST)
        elif axis_index == 1:
            result = result.at[:, layer_index].add(part_value)
            result = result + jnp.einsum('m,ike->imke', slope_row, part_slope, precision=HIGHEST)
        else:
            result = result.at[:, :, layer_index].add(part_value)
            result = result + jnp.einsum('m,ije->ijme', slope_row, part_slope, precision=HIGHEST)
    return result

def volume_term(nodal_field, elem_size, weight_cube, derivative):
    cube_scale = weight_cube[:, :, :, None] * elem_size
    grad_x = jnp.einsum('im,mjke->ijke', derivative, nodal_field, precision=HIGHEST) * cube_scale
    grad_y = jnp.einsum('jm,imke->ijke', derivative, nodal_field, precision=HIGHEST) * cube_scale
    grad_z = jnp.einsum('km,ijme->ijke', derivative, nodal_field, precision=HIGHEST) * cube_scale
    result = jnp.einsum('mi,mjke->ijke', derivative, grad_x, precision=HIGHEST)
    result = result + jnp.einsum('mj,imke->ijke', derivative, grad_y, precision=HIGHEST)
    return result + jnp.einsum('mk,ijme->ijke', derivative, grad_z, precision=HIGHEST)

def onto_mortar(face_nodes, rec_sub, halves):
    whole_face = rec_sub >= 4
    first_bit = rec_sub % 2
    second_bit = rec_sub // 2 % 2
    lower_half = jnp.einsum('ij,jkr->ikr', halves[0], face_nodes, precision=HIGHEST)
    upper_half = jnp.einsum('ij,jkr->ikr', halves[1], face_nodes, precision=HIGHEST)
    face_nodes = jnp.where(whole_face, face_nodes, jnp.where(first_bit == 0, lower_half, upper_half))
    lower_half = jnp.einsum('kj,ijr->ikr', halves[0], face_nodes, precision=HIGHEST)
    upper_half = jnp.einsum('kj,ijr->ikr', halves[1], face_nodes, precision=HIGHEST)
    return jnp.where(whole_face, face_nodes, jnp.where(second_bit == 0, lower_half, upper_half))

def off_mortar(face_nodes, rec_sub, halves):
    whole_face = rec_sub >= 4
    first_bit = rec_sub % 2
    second_bit = rec_sub // 2 % 2
    lower_half = jnp.einsum('jk,ijr->ikr', halves[0], face_nodes, precision=HIGHEST)
    upper_half = jnp.einsum('jk,ijr->ikr', halves[1], face_nodes, precision=HIGHEST)
    face_nodes = jnp.where(whole_face, face_nodes, jnp.where(second_bit == 0, lower_half, upper_half))
    lower_half = jnp.einsum('ji,jkr->ikr', halves[0], face_nodes, precision=HIGHEST)
    upper_half = jnp.einsum('ji,jkr->ikr', halves[1], face_nodes, precision=HIGHEST)
    return jnp.where(whole_face, face_nodes, jnp.where(first_bit == 0, lower_half, upper_half))

def mortar_traces(face_value, face_slope, rec_col, rec_sub, halves):
    record_total = rec_col.shape[0]
    value_part = onto_mortar(face_value[:, rec_col].reshape(6, 6, record_total), rec_sub, halves)
    slope_part = onto_mortar(face_slope[:, rec_col].reshape(6, 6, record_total), rec_sub, halves)
    return jnp.concatenate([value_part.reshape(36, record_total), slope_part.reshape(36, record_total)], axis=0)

def mortar_terms(own_traces, partner, is_bound, mortar_size, live_rec, face_weight):
    own_value = own_traces[:36]
    own_slope = own_traces[36:]
    part_value = jnp.where(is_bound, 0.0, partner[:36])
    part_slope = jnp.where(is_bound, -own_slope, partner[36:])
    jump_value = own_value - part_value
    flux_value = 0.5 * (own_slope - part_slope)
    adjoint = jnp.where(is_bound, 1.0, 0.5)
    area_scale = mortar_size * mortar_size
    weight_live = face_weight[:, None] * live_rec
    term_value = weight_live * (PENALTY * mortar_size * jump_value - area_scale * flux_value)
    term_slope = -weight_live * adjoint * area_scale * jump_value
    return (term_value, term_slope)

def scatter_faces(term_value, term_slope, rec_col, rec_sub, halves, column_count):
    record_total = rec_col.shape[0]
    back_value = off_mortar(term_value.reshape(6, 6, record_total), rec_sub, halves).reshape(36, record_total)
    back_slope = off_mortar(term_slope.reshape(6, 6, record_total), rec_sub, halves).reshape(36, record_total)
    face_value = jnp.zeros((36, column_count), jnp.float32).at[:, rec_col].add(back_value)
    face_slope = jnp.zeros((36, column_count), jnp.float32).at[:, rec_col].add(back_slope)
    return (face_value, face_slope)

def reference(rhs, start, spectrum_top, elem_code, rec_elem, rec_dir, rec_sub, rec_peer, rec_index, send_rec):
    weights, derivative, halves, stiff_diag = float_tables()
    elem_total = rhs.shape[1]
    record_total = rec_elem.shape[0]
    elem_dev = elem_total // N_PARTS
    rec_dev = record_total // N_PARTS
    capacity = send_rec.shape[0] // (N_PARTS * N_PARTS)
    owner_device = jnp.arange(record_total, dtype=jnp.int32) // rec_dev
    global_elem = owner_device * elem_dev + rec_elem
    rec_col = rec_dir * elem_total + global_elem
    code_float = elem_code.astype(jnp.float32)
    elem_size = 0.5 * code_float
    inv_size = jnp.where(elem_code > 0, 2.0 / jnp.maximum(code_float, 1.0), 0.0)
    live_elem = elem_code > 0
    own_size = elem_size[global_elem]
    mortar_size = jnp.where(rec_sub < 4, 0.5 * own_size, own_size)
    live_rec = (rec_sub < 5).astype(jnp.float32)
    is_bound = rec_peer < 0
    is_local = rec_peer == owner_device
    is_remote = jnp.logical_and(jnp.logical_not(is_bound), jnp.logical_not(is_local))
    safe_peer = jnp.maximum(rec_peer, 0)
    link_slot = jnp.where(is_remote, (safe_peer * N_PARTS + owner_device) * capacity + rec_index, 0)
    partner_index = jnp.where(is_remote, safe_peer * rec_dev + send_rec[link_slot], safe_peer * rec_dev + rec_index)
    weight_cube = weights[:, None, None] * weights[None, :, None] * weights[None, None, :]
    face_weight = (weights[:, None] * weights[None, :]).reshape(36)
    precond_scale = inv_size[None, :] / stiff_diag[:, None]

    def apply_operator(flat_field):
        nodal_field = flat_field.reshape(6, 6, 6, elem_total)
        face_value, face_slope = face_traces(nodal_field, inv_size, derivative)
        own_traces = mortar_traces(face_value, face_slope, rec_col, rec_sub, halves)
        volume = volume_term(nodal_field, elem_size, weight_cube, derivative)
        partner = own_traces[:, partner_index]
        term_value, term_slope = mortar_terms(own_traces, partner, is_bound, mortar_size, live_rec, face_weight)
        res_value, res_slope = scatter_faces(term_value, term_slope, rec_col, rec_sub, halves, 6 * elem_total)
        lifted = lift_faces(res_value, res_slope, inv_size, derivative, elem_total)
        return (volume + lifted).reshape(216, elem_total)
    scale_total = 216.0 * elem_total

    def residual_of(solution):
        return jnp.where(live_elem[None, :], rhs - apply_operator(solution), 0.0)

    def log_norms(residual, precond):
        total_sums = jnp.stack([jnp.sum(residual * residual), jnp.sum(residual * precond)])
        return 0.5 * jnp.log(total_sums / scale_total)
    top_value = spectrum_top[0]
    bottom = top_value / BOTTOM_RATIO
    center = 0.5 * (top_value + bottom)
    radius = 0.5 * (top_value - bottom)
    sigma_ratio = center / radius
    rho_prev = 1.0 / sigma_ratio
    solution = start
    residual = residual_of(solution)
    precond = precond_scale * residual
    direction = precond / center
    rows_list = [log_norms(residual, precond)]
    for step_index in range(1, ITERS):
        solution = solution + direction
        residual = residual_of(solution)
        precond = precond_scale * residual
        rows_list.append(log_norms(residual, precond))
        rho_next = 1.0 / (2.0 * sigma_ratio - rho_prev)
        direction = rho_next * rho_prev * direction + 2.0 * rho_next / radius * precond
        rho_prev = rho_next
    solution = solution + direction
    return (solution, jnp.stack(rows_list))
```

```python
import functools
import math

import jax
import jax.numpy as jnp
import numpy as np
from jax import lax
from jax.experimental import pallas as pl
from jax.experimental.pallas import tpu as pltpu
from jax.sharding import PartitionSpec as P

LD = 4
ITERS = 3


PENALTY = 36.0
BOTTOM_RATIO = 8.0


def lobatto_tables():
    root_seven = math.sqrt(7.0)
    inner_root = math.sqrt(1.0 / 3.0 - 2.0 * root_seven / 21.0)
    outer_root = math.sqrt(1.0 / 3.0 + 2.0 * root_seven / 21.0)
    points = (np.array([-1.0, -outer_root, -inner_root, inner_root, outer_root, 1.0]) + 1.0) / 2.0
    weights = (
        np.array(
            [
                1.0 / 15.0,
                (14.0 - root_seven) / 30.0,
                (14.0 + root_seven) / 30.0,
                (14.0 + root_seven) / 30.0,
                (14.0 - root_seven) / 30.0,
                1.0 / 15.0,
            ]
        )
        / 2.0
    )
    barycentric = np.array(
        [1.0 / np.prod([points[j] - points[k] for k in range(6) if k != j]) for j in range(6)]
    )
    derivative = np.zeros((6, 6))
    for i in range(6):
        for j in range(6):
            if i != j:
                derivative[i, j] = barycentric[j] / barycentric[i] / (points[i] - points[j])
        derivative[i, i] = -np.sum(derivative[i])
    halves = np.zeros((2, 6, 6))
    for which_half in range(2):
        targets = (points + which_half) / 2.0
        for i in range(6):
            for j in range(6):
                halves[which_half, i, j] = np.prod(
                    [(targets[i] - points[k]) / (points[j] - points[k]) for k in range(6) if k != j]
                )
    column_sums = np.sum(derivative * derivative * weights[:, None], axis=0)
    stiff_diag = (
        column_sums[:, None, None] * weights[None, :, None] * weights[None, None, :]
        + weights[:, None, None] * column_sums[None, :, None] * weights[None, None, :]
        + weights[:, None, None] * weights[None, :, None] * column_sums[None, None, :]
    )
    return (weights, derivative, halves, stiff_diag.reshape(216))


BF16 = jnp.bfloat16
F32 = jnp.float32


def split_np(matrix):
    high = np.asarray(matrix, np.float32).astype(BF16)
    low = (np.asarray(matrix, np.float64) - high.astype(np.float64)).astype(np.float32).astype(BF16)
    return high, low


def operators():
    weights, derivative, halves, stiff_diag = lobatto_tables()
    eye = np.eye(6)
    trace_rows = []
    for direction in range(6):
        axis_index = direction // 2
        layer_index = 5 * (direction % 2)
        orientation = 2.0 * (direction % 2) - 1.0
        for row in (eye[layer_index], orientation * derivative[layer_index]):
            factors = [eye, eye, eye]
            factors[axis_index] = row[None, :]
            trace_rows.append(np.kron(np.kron(factors[0], factors[1]), factors[2]))
    traces = np.concatenate(trace_rows, axis=0)
    stiff_1d = derivative.T @ (weights[:, None] * derivative)
    mass = np.diag(weights)
    stiffness = (
        np.kron(np.kron(stiff_1d, mass), mass)
        + np.kron(np.kron(mass, stiff_1d), mass)
        + np.kron(np.kron(mass, mass), stiff_1d)
    )
    blocks = []
    for sub in range(4):
        quarter = np.kron(halves[sub % 2], halves[sub // 2])
        blocks.append(np.kron(np.eye(2), quarter))
    return traces, stiffness, np.concatenate(blocks, axis=0), np.outer(weights, weights).reshape(36, 1), stiff_diag


def split(value):
    high = value.astype(BF16)
    return high, (value - high.astype(F32)).astype(BF16)


def dot(left, right):
    return jnp.dot(left, right, preferred_element_type=F32)


def dot3(left_high, left_low, right):
    high, low = split(right)
    return dot(left_high, high) + (dot(left_high, low) + dot(left_low, high))


def one_hot(index_row, rows, base=0):
    count = index_row.shape[1]
    position = lax.broadcasted_iota(jnp.int32, (rows, count), 0)
    return jnp.where(position == index_row - base, 1.0, 0.0).astype(BF16)


def pick(traces, elem, direction, sub, onto):
    wide = dot(traces, one_hot(elem, traces.shape[1]))
    face = jnp.zeros((72, elem.shape[1]), F32)
    for d in range(6):
        both = wide[72 * d : 72 * d + 72] + wide[432 + 72 * d : 432 + 72 * d + 72]
        face = jnp.where(direction == d, both, face)
    high, low = split(face)
    quarters = dot(onto, jnp.concatenate([high, low, high], axis=0))
    result = face
    for s in range(4):
        result = jnp.where(sub == s, quarters[72 * s : 72 * s + 72], result)
    return result


def send_kernel(x_ref, inv_ref, code_ref, mat_high, mat_low, onto_ref, out_ref, traces_ref):
    @pl.when(pl.program_id(0) == 0)
    def _():
        raw = dot3(mat_high[...], mat_low[...], x_ref[...])
        row = lax.broadcasted_iota(jnp.int32, raw.shape, 0)
        raw = jnp.where(lax.rem(row, 72) >= 36, raw * inv_ref[...], raw)
        high, low = split(raw)
        traces_ref[0:432] = high
        traces_ref[432:864] = low

    code = code_ref[...]
    out_ref[...] = pick(traces_ref[...], code[0:1], code[1:2], code[2:3], onto_ref[...])


def exchange_kernel(steps, axis, capacity, src_ref, dst_ref, send_sem, recv_sem):
    count = lax.axis_size(axis)
    me = lax.axis_index(axis)
    barrier = pltpu.get_barrier_semaphore()
    peers = [lax.rem(me + step + count, count) for step in steps]
    for peer in peers:
        pl.semaphore_signal(barrier, inc=1, device_id=(peer,), device_id_type=pl.DeviceIdType.MESH)
    pl.semaphore_wait(barrier, len(steps))
    copies = []
    for k, peer in enumerate(peers):
        part = pl.ds(k * capacity, capacity)
        copy = pltpu.make_async_remote_copy(
            src_ref=src_ref.at[:, part],
            dst_ref=dst_ref.at[:, part],
            send_sem=send_sem.at[k],
            recv_sem=recv_sem.at[k],
            device_id=(peer,),
            device_id_type=pl.DeviceIdType.MESH,
        )
        copy.start()
        copies.append(copy)
    for copy in copies:
        copy.wait()


def apply_kernel(
    coef_ref, x_ref, dirn_ref, rhs_ref, elem_ref, prec_ref, traces_ref, recv_ref, code_ref, rows_ref,
    size_ref, onto_ref, off_ref, weight_ref, stiff_high, stiff_low, lift_high, lift_low,
    x_out, dirn_out, sums_out, pool, total,
):
    chunk = pool.shape[2]

    @pl.when(pl.program_id(0) == 0)
    def _():
        for k in range(pool.shape[0]):
            high, low = split(recv_ref[:, k * chunk : (k + 1) * chunk])
            pool[k, 0:72] = high
            pool[k, 72:144] = low
        total[...] = jnp.zeros_like(total)

    code = code_ref[...]
    elem, direction, sub = code[0:1], code[1:2], code[2:3]
    bound = code[6:7] > 0
    width = elem.shape[1]
    own = pick(traces_ref[...], elem, direction, sub, onto_ref[...])
    near = pick(traces_ref[...], code[3:4], code[4:5], code[5:6], onto_ref[...])

    def far_step(k, carry):
        return carry + dot(pool[k], one_hot(code[7:8], chunk, k * chunk))

    far = lax.fori_loop(0, pool.shape[0], far_step, jnp.zeros((144, width), F32))
    partner = near + (far[0:72] + far[72:144])
    own_value, own_slope = own[0:36], own[36:72]
    part_value = jnp.where(bound, 0.0, partner[0:36])
    part_slope = jnp.where(bound, -own_slope, partner[36:72])
    jump = own_value - part_value
    flux = 0.5 * (own_slope - part_slope)
    mortar = size_ref[0:1]
    area = mortar * mortar
    weight = weight_ref[...] * size_ref[1:2]
    term_value = weight * (PENALTY * mortar * jump - area * flux)
    term_slope = -weight * (jnp.where(bound, 1.0, 0.5) * area) * jump
    terms = jnp.concatenate([term_value, term_slope], axis=0)
    spread = jnp.concatenate([jnp.where(sub == s, terms, 0.0) for s in range(4)], axis=0)
    spread_high, spread_low = split(spread)
    back = dot(off_ref[...], jnp.concatenate([spread_high, spread_low, spread_high], axis=0))
    back = jnp.where(sub >= 4, terms, back)
    wide = jnp.concatenate([jnp.where(direction == d, back, 0.0) for d in range(6)], axis=0)
    wide_high, wide_low = split(wide)
    lanes = lax.broadcasted_iota(jnp.int32, (width, total.shape[1]), 1)
    hot = jnp.where(lanes == rows_ref[...], 1.0, 0.0).astype(BF16)
    total[...] += dot(wide_high, hot) + dot(wide_low, hot)

    @pl.when(pl.program_id(0) == pl.num_programs(0) - 1)
    def _():
        size, inv = elem_ref[0:1], elem_ref[1:2]
        field = x_ref[...]
        row = lax.broadcasted_iota(jnp.int32, total.shape, 0)
        faces = jnp.where(lax.rem(row, 72) >= 36, total[...] * inv, total[...])
        applied = size * dot3(stiff_high[...], stiff_low[...], field)
        applied = applied + dot3(lift_high[...], lift_low[...], faces)
        residual = jnp.where(size > 0.0, rhs_ref[...] - applied, 0.0)
        scaled = residual * (inv * prec_ref[...])
        step = coef_ref[0] * dirn_ref[...] + coef_ref[1] * scaled
        dirn_out[...] = step
        x_out[...] = field + step
        sums_out[0:1] = jnp.sum(residual * residual, axis=0, keepdims=True)
        sums_out[1:2] = jnp.sum(residual * scaled, axis=0, keepdims=True)


def take_small(tables, index):
    rows = tables.shape[1] // 128
    fine = (jnp.arange(128, dtype=jnp.int32)[:, None] == (index % 128)[None, :]).astype(BF16)
    wide = jnp.dot(tables.reshape(-1, 128).astype(BF16), fine, preferred_element_type=F32)
    wide = wide.reshape(tables.shape[0], rows, -1)
    coarse = jnp.arange(rows, dtype=jnp.int32)[:, None] == (index // 128)[None, :]
    return jnp.sum(jnp.where(coarse[None], wide, 0.0), axis=1).astype(jnp.int32)


def tile(count):
    for width in (512, 256, 128):
        if count % width == 0:
            return width
    return count


def whole(shape):
    return pl.BlockSpec(shape, lambda i: (0,) * len(shape))


def on_device(
    rhs, start, spectrum_top, elem_code, rec_elem, rec_dir, rec_sub, rec_peer, rec_index, send_rec
):
    traces, stiffness, interp, face_weight, stiff_diag = operators()
    part_count = lax.axis_size("parts")
    own_index = lax.axis_index("parts")
    elem_count = rhs.shape[1]
    record_count = rec_elem.shape[0]
    capacity = send_rec.shape[0] // part_count
    far_reach = 2 * LD - 1
    code_float = elem_code.astype(F32)
    elem_size = 0.5 * code_float
    inv_size = jnp.where(elem_code > 0, 2.0 / jnp.maximum(code_float, 1.0), 0.0)
    elem_rows = jnp.stack([elem_size, inv_size])
    is_bound = rec_peer < 0
    is_local = rec_peer == own_index
    is_remote = jnp.logical_and(jnp.logical_not(is_bound), jnp.logical_not(is_local))
    offset = own_index - rec_peer
    position = jnp.where(offset < 0, offset + far_reach, offset + far_reach - 1)
    remote_col = jnp.where(is_remote, position * capacity + rec_index, -1)
    steps = list(range(-far_reach, 0)) + list(range(1, far_reach + 1))
    lists = send_rec.reshape(part_count, capacity)
    lists = jnp.concatenate([lists[part_count - far_reach :], lists, lists[:far_reach]], axis=0)
    lists = lax.dynamic_slice_in_dim(lists, own_index, 2 * far_reach + 1, 0)
    send_cols = jnp.concatenate([lists[:far_reach], lists[far_reach + 1 :]], axis=0).reshape(-1)
    send_count = send_cols.shape[0]

    own_size = 0.5 * take_small(elem_code[None], rec_elem)[0].astype(F32)
    mortar_size = jnp.where(rec_sub < 4, 0.5 * own_size, own_size)
    size_rows = jnp.stack([mortar_size, (rec_sub < 5).astype(F32)])
    tables = jnp.stack([rec_elem // 256, rec_elem % 256, rec_dir * 8 + rec_sub])
    found = take_small(tables, jnp.concatenate([send_cols, rec_index]))
    found = jnp.stack([found[0] * 256 + found[1], found[2] // 8, found[2] % 8])
    send_code = found[:, :send_count]
    near = jnp.where(is_local[None], found[:, send_count:], -1)
    rec_code = jnp.concatenate(
        [jnp.stack([rec_elem, rec_dir, rec_sub]), near, is_bound.astype(jnp.int32)[None], remote_col[None]],
        axis=0,
    )
    rec_rows = rec_elem[:, None]

    mat_high, mat_low = split_np(traces)
    lift_high, lift_low = split_np(traces.T)
    stiff_high, stiff_low = split_np(stiffness)
    onto_high, onto_low = split_np(interp)
    onto = np.concatenate([onto_high, onto_high, onto_low], axis=1)
    flat = np.concatenate([interp[72 * s : 72 * s + 72].T for s in range(4)], axis=1)
    off_high, off_low = split_np(flat)
    off = np.concatenate([off_high, off_high, off_low], axis=1)
    prec = jnp.asarray((1.0 / stiff_diag).reshape(216, 1), F32)
    weight = jnp.asarray(face_weight, F32)

    send_tile, rec_tile, chunk = tile(send_count), tile(record_count), tile(send_count)
    params = pltpu.CompilerParams(vmem_limit_bytes=60 * 1024 * 1024)
    field = (216, elem_count)

    def send_call(x):
        return pl.pallas_call(
            send_kernel,
            grid=(send_count // send_tile,),
            in_specs=[
                whole(field),
                whole((1, elem_count)),
                pl.BlockSpec((3, send_tile), lambda i: (0, i)),
                whole((432, 216)),
                whole((432, 216)),
                whole((288, 216)),
            ],
            out_specs=[pl.BlockSpec((72, send_tile), lambda i: (0, i)), whole((864, elem_count))],
            out_shape=[
                jax.ShapeDtypeStruct((72, send_count), F32),
                jax.ShapeDtypeStruct((864, elem_count), BF16),
            ],
            compiler_params=params,
            name="send_traces",
        )(x, inv_size[None], send_code, jnp.asarray(mat_high), jnp.asarray(mat_low), jnp.asarray(onto))

    def exchange(outgoing):
        return pl.pallas_call(
            functools.partial(exchange_kernel, steps, "parts", capacity),
            in_specs=[pl.BlockSpec(memory_space=pl.ANY)],
            out_specs=pl.BlockSpec(memory_space=pl.ANY),
            out_shape=jax.ShapeDtypeStruct((72, send_count), F32),
            scratch_shapes=[
                pltpu.SemaphoreType.DMA((len(steps),)),
                pltpu.SemaphoreType.DMA((len(steps),)),
            ],
            compiler_params=pltpu.CompilerParams(collective_id=0, has_side_effects=True),
            name="exchange",
        )(outgoing)

    def apply_call(coef, x, dirn, element_traces, received):
        return pl.pallas_call(
            apply_kernel,
            grid=(record_count // rec_tile,),
            in_specs=[
                pl.BlockSpec(memory_space=pltpu.SMEM),
                whole(field),
                whole(field),
                whole(field),
                whole((2, elem_count)),
                whole((216, 1)),
                whole((864, elem_count)),
                whole((72, send_count)),
                pl.BlockSpec((8, rec_tile), lambda i: (0, i)),
                pl.BlockSpec((rec_tile, 1), lambda i: (i, 0)),
                pl.BlockSpec((2, rec_tile), lambda i: (0, i)),
                whole((288, 216)),
                whole((72, 864)),
                whole((36, 1)),
                whole((216, 216)),
                whole((216, 216)),
                whole((216, 432)),
                whole((216, 432)),
            ],
            out_specs=[whole(field), whole(field), whole((2, elem_count))],
            out_shape=[
                jax.ShapeDtypeStruct(field, F32),
                jax.ShapeDtypeStruct(field, F32),
                jax.ShapeDtypeStruct((2, elem_count), F32),
            ],
            scratch_shapes=[
                pltpu.VMEM((send_count // chunk, 144, chunk), BF16),
                pltpu.VMEM((432, elem_count), F32),
            ],
            compiler_params=params,
            name="apply_operator",
        )(
            coef, x, dirn, rhs, elem_rows, prec, element_traces, received, rec_code, rec_rows, size_rows,
            jnp.asarray(onto), jnp.asarray(off), weight,
            jnp.asarray(stiff_high), jnp.asarray(stiff_low), jnp.asarray(lift_high), jnp.asarray(lift_low),
        )

    scale_total = 216.0 * elem_count * part_count
    top_value = spectrum_top[0]
    bottom = top_value / BOTTOM_RATIO
    center = 0.5 * (top_value + bottom)
    radius = 0.5 * (top_value - bottom)
    sigma_ratio = center / radius
    rho_prev = 1.0 / sigma_ratio
    coef = jnp.stack([jnp.zeros_like(center), 1.0 / center])
    x, dirn, partials = start, start, []
    for step_index in range(ITERS):
        if step_index:
            rho_next = 1.0 / (2.0 * sigma_ratio - rho_prev)
            coef = jnp.stack([rho_next * rho_prev, 2.0 * rho_next / radius])
            rho_prev = rho_next
        outgoing, element_traces = send_call(x)
        received = exchange(outgoing)
        x, dirn, sums = apply_call(coef, x, dirn, element_traces, received)
        partials.append(jnp.sum(sums, axis=1))
    norms = 0.5 * jnp.log(lax.psum(jnp.stack(partials), "parts") / scale_total)
    return (x, norms)


def solution(mesh):
    placed = (
        P(None, "parts"),
        P(None, "parts"),
        P(),
        P("parts"),
        P("parts"),
        P("parts"),
        P("parts"),
        P("parts"),
        P("parts"),
        P("parts"),
    )
    return jax.shard_map(
        on_device, mesh=mesh, in_specs=placed, out_specs=(P(None, "parts"), P()), check_vma=False
    )
```

```python
import functools
import math

import jax
import jax.numpy as jnp
import numpy as np
from jax import lax
from jax.experimental import pallas as pl
from jax.experimental.pallas import tpu as pltpu
from jax.sharding import PartitionSpec as P

LD = 4
ITERS = 3


PENALTY = 36.0
BOTTOM_RATIO = 8.0


def lobatto_tables():
    root_seven = math.sqrt(7.0)
    inner_root = math.sqrt(1.0 / 3.0 - 2.0 * root_seven / 21.0)
    outer_root = math.sqrt(1.0 / 3.0 + 2.0 * root_seven / 21.0)
    points = (np.array([-1.0, -outer_root, -inner_root, inner_root, outer_root, 1.0]) + 1.0) / 2.0
    weights = (
        np.array(
            [
                1.0 / 15.0,
                (14.0 - root_seven) / 30.0,
                (14.0 + root_seven) / 30.0,
                (14.0 + root_seven) / 30.0,
                (14.0 - root_seven) / 30.0,
                1.0 / 15.0,
            ]
        )
        / 2.0
    )
    barycentric = np.array(
        [1.0 / np.prod([points[j] - points[k] for k in range(6) if k != j]) for j in range(6)]
    )
    derivative = np.zeros((6, 6))
    for i in range(6):
        for j in range(6):
            if i != j:
                derivative[i, j] = barycentric[j] / barycentric[i] / (points[i] - points[j])
        derivative[i, i] = -np.sum(derivative[i])
    halves = np.zeros((2, 6, 6))
    for which_half in range(2):
        targets = (points + which_half) / 2.0
        for i in range(6):
            for j in range(6):
                halves[which_half, i, j] = np.prod(
                    [(targets[i] - points[k]) / (points[j] - points[k]) for k in range(6) if k != j]
                )
    column_sums = np.sum(derivative * derivative * weights[:, None], axis=0)
    stiff_diag = (
        column_sums[:, None, None] * weights[None, :, None] * weights[None, None, :]
        + weights[:, None, None] * column_sums[None, :, None] * weights[None, None, :]
        + weights[:, None, None] * weights[None, :, None] * column_sums[None, None, :]
    )
    return (weights, derivative, halves, stiff_diag.reshape(216))


BF16 = jnp.bfloat16
F32 = jnp.float32


def split_np(matrix):
    high = np.asarray(matrix, np.float32).astype(BF16)
    low = (np.asarray(matrix, np.float64) - high.astype(np.float64)).astype(np.float32).astype(BF16)
    return high, low


def operators():
    weights, derivative, halves, stiff_diag = lobatto_tables()
    eye = np.eye(6)
    trace_rows = []
    for direction in range(6):
        axis_index = direction // 2
        layer_index = 5 * (direction % 2)
        orientation = 2.0 * (direction % 2) - 1.0
        for row in (eye[layer_index], orientation * derivative[layer_index]):
            factors = [eye, eye, eye]
            factors[axis_index] = row[None, :]
            trace_rows.append(np.kron(np.kron(factors[0], factors[1]), factors[2]))
    traces = np.concatenate(trace_rows, axis=0)
    stiff_1d = derivative.T @ (weights[:, None] * derivative)
    mass = np.diag(weights)
    stiffness = (
        np.kron(np.kron(stiff_1d, mass), mass)
        + np.kron(np.kron(mass, stiff_1d), mass)
        + np.kron(np.kron(mass, mass), stiff_1d)
    )
    blocks = []
    for sub in range(4):
        quarter = np.kron(halves[sub % 2], halves[sub // 2])
        blocks.append(np.kron(np.eye(2), quarter))
    return traces, stiffness, np.concatenate(blocks, axis=0), np.outer(weights, weights).reshape(36, 1), stiff_diag


def split(value):
    high = value.astype(BF16)
    return high, (value - high.astype(F32)).astype(BF16)


def dot(left, right):
    return jnp.dot(left, right, preferred_element_type=F32)


def dot3(left_high, left_low, right):
    high, low = split(right)
    return dot(left_high, high) + (dot(left_high, low) + dot(left_low, high))


def one_hot(index_row, rows, base=0):
    count = index_row.shape[1]
    position = lax.broadcasted_iota(jnp.int32, (rows, count), 0)
    return jnp.where(position == index_row - base, 1.0, 0.0).astype(BF16)


def pick(traces, elem, direction, sub, onto):
    wide = dot(traces, one_hot(elem, traces.shape[1]))
    face = jnp.zeros((72, elem.shape[1]), F32)
    for d in range(6):
        both = wide[72 * d : 72 * d + 72] + wide[432 + 72 * d : 432 + 72 * d + 72]
        face = jnp.where(direction == d, both, face)
    high, low = split(face)
    quarters = dot(onto, jnp.concatenate([high, low, high], axis=0))
    result = face
    for s in range(4):
        result = jnp.where(sub == s, quarters[72 * s : 72 * s + 72], result)
    return result


def send_kernel(x_ref, inv_ref, code_ref, mat_high, mat_low, onto_ref, out_ref, traces_ref):
    @pl.when(pl.program_id(0) == 0)
    def _():
        raw = dot3(mat_high[...], mat_low[...], x_ref[...])
        row = lax.broadcasted_iota(jnp.int32, raw.shape, 0)
        raw = jnp.where(lax.rem(row, 72) >= 36, raw * inv_ref[...], raw)
        high, low = split(raw)
        traces_ref[0:432] = high
        traces_ref[432:864] = low

    code = code_ref[...]
    picked = pick(traces_ref[...], code[0:1], code[1:2], code[2:3], onto_ref[...])
    capacity = out_ref.shape[2]
    for k in range(out_ref.shape[0]):
        out_ref[k] = picked[:, k * capacity : (k + 1) * capacity]


def exchange_kernel(
    steps, axis, width, src_ref, x_ref, traces_ref, code_ref, onto_ref, stiff_high, stiff_low,
    dst_ref, own_ref, near_ref, volume_ref, send_sem, recv_sem,
):
    count = lax.axis_size(axis)
    me = lax.axis_index(axis)
    barrier = pltpu.get_barrier_semaphore()
    peers = [lax.rem(me + step + count, count) for step in steps]
    for peer in peers:
        pl.semaphore_signal(barrier, inc=1, device_id=(peer,), device_id_type=pl.DeviceIdType.MESH)
    pl.semaphore_wait(barrier, len(steps))
    copies = []
    for k, peer in enumerate(peers):
        copy = pltpu.make_async_remote_copy(
            src_ref=src_ref.at[k],
            dst_ref=dst_ref.at[k],
            send_sem=send_sem.at[k],
            recv_sem=recv_sem.at[k],
            device_id=(peer,),
            device_id_type=pl.DeviceIdType.MESH,
        )
        copy.start()
        copies.append(copy)

    def step_tile(i, carry):
        part = pl.ds(pl.multiple_of(i * width, width), width)
        code = code_ref[:, part]
        own_ref[:, part] = pick(traces_ref[...], code[0:1], code[1:2], code[2:3], onto_ref[...])
        near_ref[:, part] = pick(traces_ref[...], code[3:4], code[4:5], code[5:6], onto_ref[...])
        return carry

    lax.fori_loop(0, code_ref.shape[1] // width, step_tile, 0)
    volume_ref[...] = dot3(stiff_high[...], stiff_low[...], x_ref[...])
    for copy in copies:
        copy.wait()


def norms_kernel(axis, sums_ref, out_ref, landing, send_sem, recv_sem):
    count = lax.axis_size(axis)
    me = lax.axis_index(axis)
    barrier = pltpu.get_barrier_semaphore()

    def greet(k, carry):
        peer = lax.rem(me + k, count)
        pl.semaphore_signal(barrier, inc=1, device_id=(peer,), device_id_type=pl.DeviceIdType.MESH)
        return carry

    def copy_to(k):
        return pltpu.make_async_remote_copy(
            src_ref=sums_ref,
            dst_ref=landing.at[k],
            send_sem=send_sem.at[k],
            recv_sem=recv_sem.at[k],
            device_id=(lax.rem(me + k, count),),
            device_id_type=pl.DeviceIdType.MESH,
        )

    def start(k, carry):
        copy_to(k).start()
        return carry

    def finish(k, carry):
        copy_to(k).wait()
        return carry

    lax.fori_loop(1, count, greet, 0)
    pl.semaphore_wait(barrier, count - 1)
    lax.fori_loop(1, count, start, 0)
    landing[0] = sums_ref[...]
    lax.fori_loop(1, count, finish, 0)

    def add(j, total):
        return total + landing[lax.rem(me + count - j, count)]

    total = lax.fori_loop(0, count, add, jnp.zeros(out_ref.shape, F32))
    out_ref[...] = jnp.broadcast_to(jnp.sum(total, axis=1, keepdims=True), out_ref.shape)


def apply_kernel(
    row_index, coef_ref, x_ref, dirn_ref, rhs_ref, elem_ref, prec_ref, recv_ref, own_ref, near_ref,
    volume_ref, code_ref, rows_ref, size_ref, off_ref, weight_ref, lift_high, lift_low, prior_ref,
    x_out, dirn_out, sums_out, pool, total,
):
    peer_count = recv_ref.shape[0]

    @pl.when(pl.program_id(0) == 0)
    def _():
        for k in range(peer_count):
            high, low = split(recv_ref[k])
            pool[144 * k : 144 * k + 72] = high
            pool[144 * k + 72 : 144 * k + 144] = low
        total[...] = jnp.zeros_like(total)

    code = code_ref[...]
    direction, sub = code[1:2], code[2:3]
    bound = code[6:7] == -1
    width = sub.shape[1]
    own = own_ref[...]
    wide = dot(pool[...], one_hot(code[7:8], pool.shape[1]))
    partner = near_ref[...]
    for k in range(peer_count):
        both = wide[144 * k : 144 * k + 72] + wide[144 * k + 72 : 144 * k + 144]
        partner = jnp.where(code[6:7] == k, both, partner)
    own_value, own_slope = own[0:36], own[36:72]
    part_value = jnp.where(bound, 0.0, partner[0:36])
    part_slope = jnp.where(bound, -own_slope, partner[36:72])
    jump = own_value - part_value
    flux = 0.5 * (own_slope - part_slope)
    mortar = size_ref[0:1]
    area = mortar * mortar
    weight = weight_ref[...] * size_ref[1:2]
    term_value = weight * (PENALTY * mortar * jump - area * flux)
    term_slope = -weight * (jnp.where(bound, 1.0, 0.5) * area) * jump
    terms = jnp.concatenate([term_value, term_slope], axis=0)
    spread = jnp.concatenate([jnp.where(sub == s, terms, 0.0) for s in range(4)], axis=0)
    spread_high, spread_low = split(spread)
    back = dot(off_ref[...], jnp.concatenate([spread_high, spread_low, spread_high], axis=0))
    back = jnp.where(sub >= 4, terms, back)
    spread = jnp.concatenate([jnp.where(direction == d, back, 0.0) for d in range(6)], axis=0)
    wide_high, wide_low = split(spread)
    lanes = lax.broadcasted_iota(jnp.int32, (width, total.shape[1]), 1)
    hot = jnp.where(lanes == rows_ref[...], 1.0, 0.0).astype(BF16)
    total[...] += dot(wide_high, hot) + dot(wide_low, hot)

    @pl.when(pl.program_id(0) == pl.num_programs(0) - 1)
    def _():
        size, inv = elem_ref[0:1], elem_ref[1:2]
        field = x_ref[...]
        row = lax.broadcasted_iota(jnp.int32, total.shape, 0)
        faces = jnp.where(lax.rem(row, 72) >= 36, total[...] * inv, total[...])
        applied = size * volume_ref[...]
        applied = applied + dot3(lift_high[...], lift_low[...], faces)
        residual = jnp.where(size > 0.0, rhs_ref[...] - applied, 0.0)
        scaled = residual * (inv * prec_ref[...])
        step = coef_ref[0] * dirn_ref[...] + coef_ref[1] * scaled
        dirn_out[...] = step
        x_out[...] = field + step
        squares = jnp.sum(residual * residual, axis=0, keepdims=True)
        products = jnp.sum(residual * scaled, axis=0, keepdims=True)
        fold = lambda line: sum(line[:, k : k + 128] for k in range(0, line.shape[1], 128))
        row = lax.broadcasted_iota(jnp.int32, sums_out.shape, 0)
        later = jnp.where(row == 2 * row_index + 1, fold(products), prior_ref[...])
        sums_out[...] = jnp.where(row == 2 * row_index, fold(squares), later)


def take_small(tables, index):
    rows = tables.shape[1] // 128
    fine = (jnp.arange(128, dtype=jnp.int32)[:, None] == (index % 128)[None, :]).astype(BF16)
    wide = jnp.dot(tables.reshape(-1, 128).astype(BF16), fine, preferred_element_type=F32)
    wide = wide.reshape(tables.shape[0], rows, -1)
    coarse = jnp.arange(rows, dtype=jnp.int32)[:, None] == (index // 128)[None, :]
    return jnp.sum(jnp.where(coarse[None], wide, 0.0), axis=1).astype(jnp.int32)


def tile(count):
    for width in (512, 256, 128):
        if count % width == 0:
            return width
    return count


def whole(shape):
    return pl.BlockSpec(shape, lambda i: (0,) * len(shape))


def on_device(
    rhs, start, spectrum_top, elem_code, rec_elem, rec_dir, rec_sub, rec_peer, rec_index, send_rec
):
    traces, stiffness, interp, face_weight, stiff_diag = operators()
    part_count = lax.axis_size("parts")
    own_index = lax.axis_index("parts")
    elem_count = rhs.shape[1]
    record_count = rec_elem.shape[0]
    capacity = send_rec.shape[0] // part_count
    far_reach = 2 * LD - 1
    code_float = elem_code.astype(F32)
    elem_size = 0.5 * code_float
    inv_size = jnp.where(elem_code > 0, 2.0 / jnp.maximum(code_float, 1.0), 0.0)
    elem_rows = jnp.stack([elem_size, inv_size])
    is_bound = rec_peer < 0
    is_local = rec_peer == own_index
    is_remote = jnp.logical_and(jnp.logical_not(is_bound), jnp.logical_not(is_local))
    offset = own_index - rec_peer
    position = jnp.where(offset < 0, offset + far_reach, offset + far_reach - 1)
    block = jnp.where(is_remote, position, jnp.where(is_bound, -1, -2))
    steps = list(range(-far_reach, 0)) + list(range(1, far_reach + 1))
    lists = send_rec.reshape(part_count, capacity)
    lists = jnp.concatenate([lists[part_count - far_reach :], lists, lists[:far_reach]], axis=0)
    lists = lax.dynamic_slice_in_dim(lists, own_index, 2 * far_reach + 1, 0)
    send_cols = jnp.concatenate([lists[:far_reach], lists[far_reach + 1 :]], axis=0).reshape(-1)
    send_count = send_cols.shape[0]

    own_size = 0.5 * take_small(elem_code[None], rec_elem)[0].astype(F32)
    mortar_size = jnp.where(rec_sub < 4, 0.5 * own_size, own_size)
    size_rows = jnp.stack([mortar_size, (rec_sub < 5).astype(F32)])
    tables = jnp.stack([rec_elem // 256, rec_elem % 256, rec_dir * 8 + rec_sub])
    found = take_small(tables, jnp.concatenate([send_cols, rec_index]))
    found = jnp.stack([found[0] * 256 + found[1], found[2] // 8, found[2] % 8])
    send_code = found[:, :send_count]
    near = jnp.where(is_local[None], found[:, send_count:], -1)
    rec_code = jnp.concatenate(
        [jnp.stack([rec_elem, rec_dir, rec_sub]), near, block[None], rec_index[None]],
        axis=0,
    )
    rec_rows = rec_elem[:, None]

    mat_high, mat_low = split_np(traces)
    lift_high, lift_low = split_np(traces.T)
    stiff_high, stiff_low = split_np(stiffness)
    onto_high, onto_low = split_np(interp)
    onto = np.concatenate([onto_high, onto_high, onto_low], axis=1)
    flat = np.concatenate([interp[72 * s : 72 * s + 72].T for s in range(4)], axis=1)
    off_high, off_low = split_np(flat)
    off = np.concatenate([off_high, off_high, off_low], axis=1)
    prec = jnp.asarray((1.0 / stiff_diag).reshape(216, 1), F32)
    weight = jnp.asarray(face_weight, F32)

    send_tile, rec_tile, peer_count = 2 * capacity, tile(record_count), len(steps)
    params = pltpu.CompilerParams(vmem_limit_bytes=60 * 1024 * 1024)
    field = (216, elem_count)

    def send_call(x):
        return pl.pallas_call(
            send_kernel,
            grid=(send_count // send_tile,),
            in_specs=[
                whole(field),
                whole((1, elem_count)),
                pl.BlockSpec((3, send_tile), lambda i: (0, i)),
                whole((432, 216)),
                whole((432, 216)),
                whole((288, 216)),
            ],
            out_specs=[pl.BlockSpec((2, 72, capacity), lambda i: (i, 0, 0)), whole((864, elem_count))],
            out_shape=[
                jax.ShapeDtypeStruct((peer_count, 72, capacity), F32),
                jax.ShapeDtypeStruct((864, elem_count), BF16),
            ],
            compiler_params=params,
            name="send_traces",
        )(x, inv_size[None], send_code, jnp.asarray(mat_high), jnp.asarray(mat_low), jnp.asarray(onto))

    vmem = pl.BlockSpec(memory_space=pltpu.VMEM)

    def exchange(outgoing, x, element_traces):
        return pl.pallas_call(
            functools.partial(exchange_kernel, steps, "parts", rec_tile),
            in_specs=[pl.BlockSpec(memory_space=pl.ANY)] + [vmem] * 6,
            out_specs=[pl.BlockSpec(memory_space=pl.ANY)] + [vmem] * 3,
            out_shape=[
                jax.ShapeDtypeStruct((peer_count, 72, capacity), F32),
                jax.ShapeDtypeStruct((72, record_count), F32),
                jax.ShapeDtypeStruct((72, record_count), F32),
                jax.ShapeDtypeStruct(field, F32),
            ],
            scratch_shapes=[
                pltpu.SemaphoreType.DMA((peer_count,)),
                pltpu.SemaphoreType.DMA((peer_count,)),
            ],
            compiler_params=pltpu.CompilerParams(
                collective_id=0, has_side_effects=True, vmem_limit_bytes=60 * 1024 * 1024
            ),
            name="exchange",
        )(
            outgoing, x, element_traces, rec_code, jnp.asarray(onto),
            jnp.asarray(stiff_high), jnp.asarray(stiff_low),
        )

    def all_sums(sums):
        return pl.pallas_call(
            functools.partial(norms_kernel, "parts"),
            in_specs=[vmem],
            out_specs=vmem,
            out_shape=jax.ShapeDtypeStruct((8, 128), F32),
            scratch_shapes=[
                pltpu.VMEM((part_count, 8, 128), F32),
                pltpu.SemaphoreType.DMA((part_count,)),
                pltpu.SemaphoreType.DMA((part_count,)),
            ],
            compiler_params=pltpu.CompilerParams(collective_id=1, has_side_effects=True),
            name="all_sums",
        )(sums)

    def apply_call(row_index, coef, x, dirn, received, own, near_traces, volume, sums):
        tiles = lambda rows: pl.BlockSpec((rows, rec_tile), lambda i: (0, i))
        return pl.pallas_call(
            functools.partial(apply_kernel, row_index),
            grid=(record_count // rec_tile,),
            in_specs=[
                pl.BlockSpec(memory_space=pltpu.SMEM),
                whole(field),
                whole(field),
                whole(field),
                whole((2, elem_count)),
                whole((216, 1)),
                whole((peer_count, 72, capacity)),
                tiles(72),
                tiles(72),
                whole(field),
                tiles(8),
                pl.BlockSpec((rec_tile, 1), lambda i: (i, 0)),
                tiles(2),
                whole((72, 864)),
                whole((36, 1)),
                whole((216, 432)),
                whole((216, 432)),
                whole((8, 128)),
            ],
            out_specs=[whole(field), whole(field), whole((8, 128))],
            out_shape=[
                jax.ShapeDtypeStruct(field, F32),
                jax.ShapeDtypeStruct(field, F32),
                jax.ShapeDtypeStruct((8, 128), F32),
            ],
            scratch_shapes=[
                pltpu.VMEM((144 * peer_count, capacity), BF16),
                pltpu.VMEM((432, elem_count), F32),
            ],
            compiler_params=params,
            name="apply_operator",
        )(
            coef, x, dirn, rhs, elem_rows, prec, received, own, near_traces, volume, rec_code, rec_rows,
            size_rows, jnp.asarray(off), weight, jnp.asarray(lift_high), jnp.asarray(lift_low), sums,
        )

    scale_total = 216.0 * elem_count * part_count
    top_value = spectrum_top[0]
    bottom = top_value / BOTTOM_RATIO
    center = 0.5 * (top_value + bottom)
    radius = 0.5 * (top_value - bottom)
    sigma_ratio = center / radius
    rho_prev = 1.0 / sigma_ratio
    coef = jnp.stack([jnp.zeros_like(center), 1.0 / center])
    x, dirn, sums = start, start, jnp.zeros((8, 128), F32)
    for step_index in range(ITERS):
        if step_index:
            rho_next = 1.0 / (2.0 * sigma_ratio - rho_prev)
            coef = jnp.stack([rho_next * rho_prev, 2.0 * rho_next / radius])
            rho_prev = rho_next
        outgoing, element_traces = send_call(x)
        moved = exchange(outgoing, x, element_traces)
        x, dirn, sums = apply_call(step_index, coef, x, dirn, *moved, sums)
    norms = 0.5 * jnp.log(all_sums(sums)[: 2 * ITERS, 0].reshape(ITERS, 2) / scale_total)
    return (x, norms)


def solution(mesh):
    placed = (
        P(None, "parts"),
        P(None, "parts"),
        P(),
        P("parts"),
        P("parts"),
        P("parts"),
        P("parts"),
        P("parts"),
        P("parts"),
        P("parts"),
    )
    return jax.shard_map(
        on_device, mesh=mesh, in_specs=placed, out_specs=(P(None, "parts"), P()), check_vma=False
    )
```
